32 devices in a mesh: conf: 2 (over x), virt: 16 (over z, y, core).
Axes of the slice: x: 2, y: 2, z: 4, core: 2. Of those that a mesh axis runs over, the one named last changes fastest.
Arguments:
- i_factors: float32 [32, 1024, 2048], P('conf', 'virt'), parts along dimension 0, may hold values from -0.6 to 0.6
- j_factors: float32 [4, 1024, 2048], P('conf', 'virt'), parts along dimension 0, may hold values from -0.6 to 0.6
- occ_i: float32 [32], P('conf'), parts along dimension 0, may hold values from -2 to -0.3
- occ_j: float32 [4], P('conf'), parts along dimension 0, may hold values from -2 to -0.3
- virt_energy: float32 [2048], P(('conf', 'virt')), parts along dimension 0, may hold values from 0.3 to 3
Outputs:
- density: float32 [32, 1024, 2048], P('conf', 'virt'), parts along dimension 0
The draws below stay inside these ranges and needn't reach their ends.
There are 2 independent parts, one for each index of `conf`. The reference program is written for one: setup_inputs(seed, part) draws one part's arguments, and reference() takes and returns one part's arrays. A program takes and returns all parts, laid end to end along the dimension named above; each array names one. Nothing has to cross between parts.
All inputs are finite; a program needn't handle non-finite values.
Results may differ from the reference program's by a relative error of at most 0.00005.
Values sent between devices are 32-bit elements; how exact they have to be, the bound alone decides.
A program may use at most 128 MiB of HBM per device.

```python
import jax
import jax.numpy as jnp
from jax import lax

NV = 1024
NAUX = 2048
NJ = 2
NI = 16


def level_of(own_key, extent, pieces, least, top_value):
    loudness, own = 1.0, jax.random.fold_in(own_key, 6)
    for dim, blocks in pieces:
        steps = jnp.exp(jax.random.uniform(jax.random.fold_in(own, dim), (blocks,), jnp.float32, least / len(pieces), top_value / len(pieces)))
        loudness = loudness * jnp.repeat(steps, extent[dim] // blocks).reshape([-1 if axis == dim else 1 for axis in range(len(extent))])
    return loudness


def noise(stream_key, shape, spread, most, split=(), kind=jnp.bfloat16):
    array = jax.random.normal(stream_key, shape, jnp.float32) * spread
    if len(split) > 0:
        array = level_of(stream_key, shape, split, -0.22, 0.18) * array
    return jnp.clip(array, min=-most, max=most).astype(kind)


def setup_inputs(seed: int = 0, part: int = 0) -> dict:
    seeds = jax.random.split(jax.random.key(seed), 6)
    own_keys = jax.random.split(jax.random.fold_in(seeds[5], part), 6)
    return {
        "i_factors": noise(own_keys[0], (NI, NV, NAUX), 0.09, 0.6, ((1, 16),), jnp.float32),
        "j_factors": noise(own_keys[1], (NJ, NV, NAUX), 0.09, 0.6, ((1, 16),), jnp.float32),
        "occ_i": jnp.clip(jax.random.uniform(own_keys[2], (NI,), jnp.float32, -2.0, -0.3), -2.0, -0.3),
        "occ_j": jnp.clip(jax.random.uniform(own_keys[3], (NJ,), jnp.float32, -2.0, -0.3), -2.0, -0.3),
        "virt_energy": jnp.clip(0.3 + 2.7 * jax.random.uniform(own_keys[4], (NV,), jnp.float32) ** level_of(own_keys[4], (NV,), ((0, 16),), -0.2, 0.2), 0.3, 3.0),
    }


def reference(i_factors, j_factors, occ_i, occ_j, virt_energy):
    pair = jnp.einsum("iap,jbp->ijab", i_factors, j_factors, precision=lax.Precision.HIGHEST)
    swapped = jnp.swapaxes(pair, 2, 3)
    denominator = (virt_energy[None, None, :, None] + virt_energy[None, None, None, :]
                   - occ_i[:, None, None, None] - occ_j[None, :, None, None])
    amplitude = (swapped - 2.0 * pair) / denominator
    return jnp.einsum("ijab,jbp->iap", amplitude, j_factors, precision=lax.Precision.HIGHEST)
```

```python
import functools

import jax
import jax.numpy as jnp
from jax import lax
from jax.experimental import pallas as pl
from jax.experimental.pallas import tpu as pltpu
from jax.sharding import PartitionSpec as P

LANES = 128
MESH = pl.DeviceIdType.MESH


def split(value):
    high = value.astype(jnp.bfloat16)
    low = (value - high.astype(jnp.float32)).astype(jnp.bfloat16)
    return high, low


def kernel(
    n, columns, i_ref, j_ref, row_ref, col_ref, out_ref,
    i_high, i_low, j_all, direct, x_send, x_recv, total, j_parts, amp_parts,
    local_sem, j_send_sem, j_recv_sem, x_send_sem, x_recv_sem,
):
    levels = n // 2 // columns
    me = lax.axis_index("virt")
    core = lax.rem(me, 2)
    chip = me // 2
    y = lax.rem(chip, columns)
    z = chip // columns
    rows, depth = i_ref.shape
    pair = 2 * LANES
    tall = 256
    wide = 512

    load_i = pltpu.make_async_copy(i_ref, total, local_sem.at[0])
    load_i.start()
    load_j = pltpu.make_async_copy(j_ref, j_all.at[me], local_sem.at[1])
    load_j.start()

    barrier = pltpu.get_barrier_semaphore()

    @pl.loop(1, n)
    def _(step):
        pl.semaphore_signal(
            barrier, inc=1, device_id={"virt": lax.rem(me + step, n)}, device_id_type=MESH
        )

    pl.semaphore_wait(barrier, n - 1)

    def j_copy(origin, way, device):
        return pltpu.make_async_remote_copy(
            src_ref=j_all.at[origin],
            dst_ref=j_all.at[origin],
            send_sem=j_send_sem.at[origin, way],
            recv_sem=j_recv_sem.at[origin],
            device_id={"virt": device},
            device_id_type=MESH,
        )

    def j_targets(origin, act):
        place = origin // 2
        same_core = lax.rem(origin, 2) == core
        in_column = jnp.logical_and(same_core, lax.rem(place, columns) == y)
        from_z = place // columns

        @pl.when(jnp.logical_and(in_column, jnp.logical_and(z >= from_z, z + 1 < levels)))
        def _():
            act(j_copy(origin, 0, me + 2 * columns))

        @pl.when(jnp.logical_and(in_column, jnp.logical_and(z <= from_z, z > 0)))
        def _():
            act(j_copy(origin, 1, me - 2 * columns))

        if columns == 2:
            @pl.when(in_column)
            def _():
                act(j_copy(origin, 2, me + 2 * (1 - 2 * y)))

        @pl.when(same_core)
        def _():
            act(j_copy(origin, 3, me + 1 - 2 * core))

    def x_copy(other):
        return pltpu.make_async_remote_copy(
            src_ref=x_send.at[other],
            dst_ref=x_recv.at[me],
            send_sem=x_send_sem.at[other],
            recv_sem=x_recv_sem.at[me],
            device_id={"virt": other},
            device_id_type=MESH,
        )

    def x_arrival(other):
        return pltpu.make_async_remote_copy(
            src_ref=x_send.at[other],
            dst_ref=x_recv.at[other],
            send_sem=x_send_sem.at[other],
            recv_sem=x_recv_sem.at[other],
            device_id={"virt": other},
            device_id_type=MESH,
        )

    def x_stay():
        return pltpu.make_async_copy(x_send.at[me], x_recv.at[me], local_sem.at[2])

    load_j.wait()
    j_targets(me, lambda copy: copy.start())
    load_i.wait()

    @pl.loop(0, rows // 32)
    def _(step):
        part = pl.ds(pl.multiple_of(step * 32, 32), 32)
        high, low = split(total[part, :])
        i_high[part, :] = high
        i_low[part, :] = low
        total[part, :] = jnp.zeros((32, depth), jnp.float32)

    @pl.loop(0, n)
    def _(other):
        x_send[other, pl.ds(rows, 8), :] = col_ref[...]

    def split_j(place, copies):
        per = LANES // 32

        @pl.loop(0, 2 * per)
        def _(step):
            from_rows = pl.ds(pl.multiple_of(lax.rem(step, per) * 32, 32), 32)
            high, low = split(j_all[2 * place + step // per, from_rows, :])
            base = pl.multiple_of(step * 32, 32)
            j_parts[pl.ds(base, 32), :] = high
            j_parts[pl.ds(pair + base, 32), :] = low
            if copies == 3:
                j_parts[pl.ds(2 * pair + base, 32), :] = high

    def visit(step):
        level = step // 4
        kind = lax.rem(step // 2, 2)
        sign = lax.rem(step, 2)
        distance = level - kind
        at_y = jnp.where(kind == 0, y, columns - 1 - y)

        def on(way):
            at_z = z + (1 - 2 * way) * distance
            valid = jnp.logical_and(distance >= 0, jnp.logical_and(at_z >= 0, at_z < levels))
            valid = jnp.logical_and(valid, jnp.logical_or(distance > 0, way == 0))
            if columns == 1:
                valid = jnp.logical_and(valid, kind == 0)
            return valid, at_z * columns + at_y

        return on, sign

    visits = 4 * (levels + columns - 1)

    @pl.loop(0, visits)
    def _(step):
        on, sign = visit(step)

        @pl.when(sign == 0)
        def _():
            for way in range(2):
                valid, place = on(way)
                origin = 2 * place + core

                @pl.when(jnp.logical_and(valid, origin != me))
                def _():
                    j_copy(origin, 0, me).wait_recv()
                    j_targets(origin, lambda copy: copy.start())

        valid, place = on(sign)

        @pl.when(valid)
        def _():
            j_copy(2 * place + 1 - core, 0, me).wait_recv()
            split_j(place, 2)
            lane = lax.broadcasted_iota(jnp.int32, (LANES // 2, LANES), 1)
            half = LANES // 2
            contract = (((1,), (1,)), ((), ()))

            @pl.loop(0, rows // tall)
            def _(block):
                start = pl.multiple_of(block * tall, tall)
                high, low = i_high[pl.ds(start, tall), :], i_low[pl.ds(start, tall), :]
                j_high, j_low = j_parts[pl.ds(0, pair), :], j_parts[pl.ds(pair, pair), :]
                dot = functools.partial(
                    lax.dot_general, dimension_numbers=contract,
                    preferred_element_type=jnp.float32,
                )
                block_pair = dot(high, j_high) + (dot(high, j_low) + dot(low, j_high))
                direct[place, pl.ds(start, tall), :] = block_pair
                for side in range(2):
                    for group in range(tall // LANES):
                        tile = block_pair[
                            group * LANES:(group + 1) * LANES, side * LANES:(side + 1) * LANES
                        ]
                        turned = tile.T
                        moved = pltpu.roll(turned, half, 1)
                        first = jnp.where(lane < half, turned[:half], moved[half:])
                        second = jnp.where(lane < half, moved[:half], turned[half:])
                        base = start + group * LANES
                        x_send[2 * place + side, pl.ds(base, half), :] = first
                        x_send[2 * place + side, pl.ds(base + half, half), :] = second

            for side in range(2):
                other = 2 * place + side

                @pl.when(other != me)
                def _():
                    x_copy(other).start()

                @pl.when(other == me)
                def _():
                    x_stay().start()

    @pl.loop(0, visits)
    def _(step):
        on, sign = visit(step)
        valid, place = on(sign)

        @pl.when(valid)
        def _():
            split_j(place, 3)
            for side in range(2):
                other = 2 * place + side

                @pl.when(other != me)
                def _():
                    x_arrival(other).wait_recv()

                @pl.when(other == me)
                def _():
                    x_stay().wait()

            @pl.loop(0, rows // tall)
            def _(block):
                part = pl.ds(pl.multiple_of(block * tall, tall), tall)
                for side in range(2):
                    other = 2 * place + side
                    lanes = slice(side * LANES, (side + 1) * LANES)
                    swapped = x_recv[other, part, :]
                    own = direct[place, part, lanes]
                    denominator = row_ref[part, :] + x_recv[other, pl.ds(rows, 8), :][0:1]
                    high, low = split((swapped - 2.0 * own) / denominator)
                    amp_parts[:, side * LANES:(side + 1) * LANES] = high
                    amp_parts[:, pair + side * LANES:pair + (side + 1) * LANES] = high
                    amp_parts[:, 2 * pair + side * LANES:2 * pair + (side + 1) * LANES] = low

                @pl.loop(0, depth // wide)
                def _(strip):
                    at = pl.ds(pl.multiple_of(strip * wide, wide), wide)
                    total[part, at] += jnp.dot(
                        amp_parts[...], j_parts[:, at], preferred_element_type=jnp.float32
                    )

    store = pltpu.make_async_copy(total, out_ref, local_sem.at[0])
    store.start()

    @pl.loop(0, n)
    def _(other):
        j_targets(other, lambda copy: copy.wait_send())

        @pl.when(other != me)
        def _():
            x_copy(other).wait_send()

    store.wait()


def fused(columns, i_factors, j_factors, occ_i, occ_j, virt_energy):
    n = lax.axis_size("virt")
    ni, width, depth = i_factors.shape
    nj = j_factors.shape[0]
    rows = ni * width
    row_term = (virt_energy[None, :] - occ_i[:, None]).reshape(rows, 1)
    row_term = jnp.broadcast_to(row_term, (rows, LANES))
    col_term = (virt_energy[None, :] - occ_j[:, None]).reshape(1, nj * width)
    col_term = jnp.broadcast_to(col_term, (8, LANES))
    anywhere = pl.BlockSpec(memory_space=pl.ANY)
    vmem = pl.BlockSpec(memory_space=pltpu.VMEM)
    f32, bf16 = jnp.float32, jnp.bfloat16
    dma = pltpu.SemaphoreType.DMA
    out = pl.pallas_call(
        functools.partial(kernel, n, columns),
        out_shape=jax.ShapeDtypeStruct((rows, depth), f32),
        in_specs=[anywhere, anywhere, vmem, vmem],
        out_specs=anywhere,
        scratch_shapes=[
            pltpu.VMEM((rows, depth), bf16),
            pltpu.VMEM((rows, depth), bf16),
            pltpu.VMEM((n, LANES, depth), f32),
            pltpu.VMEM((n // 2, rows, 2 * LANES), f32),
            pltpu.VMEM((n, rows + 8, LANES), f32),
            pltpu.VMEM((n, rows + 8, LANES), f32),
            pltpu.VMEM((rows, depth), f32),
            pltpu.VMEM((6 * LANES, depth), bf16),
            pltpu.VMEM((256, 6 * LANES), bf16),
            dma((3,)),
            dma((n, 4)),
            dma((n,)),
            dma((n,)),
            dma((n,)),
        ],
        compiler_params=pltpu.CompilerParams(
            collective_id=0, has_side_effects=True, vmem_limit_bytes=67043328
        ),
        name="pair_exchange",
    )(i_factors.reshape(rows, depth), j_factors.reshape(nj * width, depth), row_term, col_term)
    return out.reshape(i_factors.shape)


def transpose_blocks(pair_block, blocks):
    leading = pair_block.shape[:-2]
    height = pair_block.shape[-2]
    width = pair_block.shape[-1]
    parts = pair_block.reshape(leading + (height, blocks, height))
    moved = jnp.swapaxes(parts, -1, -3)
    return moved.reshape(leading + (height, width))


def general(i_factors, j_factors, occ_i, occ_j, virt_energy):
    blocks = lax.axis_size("virt")
    left_rows = i_factors.reshape(-1, i_factors.shape[2])
    density = jnp.zeros(i_factors.shape, jnp.float32)
    whole_energy = lax.all_gather(virt_energy, "virt", axis=0, tiled=True)
    for index in range(j_factors.shape[0]):
        whole_rows = lax.all_gather(j_factors[index], "virt", axis=0, tiled=True)
        pair_block = jnp.dot(left_rows, whole_rows.T, precision=lax.Precision.HIGHEST)
        pair_block = pair_block.reshape(i_factors.shape[0], i_factors.shape[1], whole_rows.shape[0])
        swapped = lax.all_to_all(
            transpose_blocks(pair_block, blocks), "virt", split_axis=2, concat_axis=2, tiled=True
        )
        denominator = (
            virt_energy[None, :, None]
            + whole_energy[None, None, :]
            - occ_i[:, None, None]
            - occ_j[index]
        )
        amplitude = (swapped - 2.0 * pair_block) / denominator
        density = density + jnp.einsum(
            "iab,bp->iap", amplitude, whole_rows, precision=lax.Precision.HIGHEST
        )
    return density


def chip_columns(mesh):
    group = list(mesh.devices.reshape(-1, mesh.shape["virt"])[0])
    if len(group) % 2:
        return 0
    chips = group[::2]
    heights = len({getattr(device, "coords", (0, 0, place))[2] for place, device in enumerate(chips)})
    columns, left = divmod(len(chips), heights)
    return columns if left == 0 and columns in (1, 2) else 0


def body(columns, i_factors, j_factors, occ_i, occ_j, virt_energy):
    ni, width, depth = i_factors.shape
    nj = j_factors.shape[0]
    fits = nj == 2 and nj * width == LANES and (ni * width) % 256 == 0 and depth % 512 == 0
    n = lax.axis_size("virt")
    room = 4 * ni * width * depth * 2 + 4 * n * LANES * (depth + 3 * (ni * width + 8))
    if columns and fits and room < 58 * 2**20:
        return fused(columns, i_factors, j_factors, occ_i, occ_j, virt_energy)
    return general(i_factors, j_factors, occ_i, occ_j, virt_energy)


def solution(mesh):
    placed = (
        P("conf", "virt", None),
        P("conf", "virt", None),
        P("conf"),
        P("conf"),
        P(("conf", "virt")),
    )
    return jax.shard_map(
        functools.partial(body, chip_columns(mesh)),
        mesh=mesh, in_specs=placed, out_specs=P("conf", "virt", None), check_vma=False,
    )
```

```python
import functools

import jax
import jax.numpy as jnp
from jax import lax
from jax.experimental import pallas as pl
from jax.experimental.pallas import tpu as pltpu
from jax.sharding import PartitionSpec as P

LANES = 128
MESH = pl.DeviceIdType.MESH


def split(value):
    high = value.astype(jnp.bfloat16)
    low = (value - high.astype(jnp.float32)).astype(jnp.bfloat16)
    return high, low


def kernel(
    n, columns, i_ref, j_ref, energy_ref, occ_i_ref, occ_j_ref, part_ref, amp_ref, last_j_ref,
    i_high, i_low, j_all, direct, x_send, x_recv, total, j_parts, amp_parts, row_ref,
    local_sem, j_send_sem, j_recv_sem, x_send_sem, x_recv_sem, amp_sem,
):
    levels = n // 2 // columns
    me = lax.axis_index("virt")
    core = lax.rem(me, 2)
    chip = me // 2
    y = lax.rem(chip, columns)
    z = chip // columns
    rows, depth = i_ref.shape
    pair = 2 * LANES
    tall = 256
    wide = 512

    load_i = pltpu.make_async_copy(i_ref, total, local_sem.at[0])
    load_i.start()
    load_j = pltpu.make_async_copy(j_ref, j_all.at[me], local_sem.at[1])
    load_j.start()

    barrier = pltpu.get_barrier_semaphore()

    @pl.loop(1, n)
    def _(step):
        pl.semaphore_signal(
            barrier, inc=1, device_id={"virt": lax.rem(me + step, n)}, device_id_type=MESH
        )

    pl.semaphore_wait(barrier, n - 1)

    def j_copy(origin, way, device):
        return pltpu.make_async_remote_copy(
            src_ref=j_all.at[origin],
            dst_ref=j_all.at[origin],
            send_sem=j_send_sem.at[origin, way],
            recv_sem=j_recv_sem.at[origin],
            device_id={"virt": device},
            device_id_type=MESH,
        )

    def j_targets(origin, act):
        place = origin // 2
        same_core = lax.rem(origin, 2) == core
        in_column = jnp.logical_and(same_core, lax.rem(place, columns) == y)
        from_z = place // columns

        @pl.when(jnp.logical_and(in_column, jnp.logical_and(z >= from_z, z + 1 < levels)))
        def _():
            act(j_copy(origin, 0, me + 2 * columns))

        @pl.when(jnp.logical_and(in_column, jnp.logical_and(z <= from_z, z > 0)))
        def _():
            act(j_copy(origin, 1, me - 2 * columns))

        if columns == 2:
            @pl.when(in_column)
            def _():
                act(j_copy(origin, 2, me + 2 * (1 - 2 * y)))

        @pl.when(same_core)
        def _():
            act(j_copy(origin, 3, me + 1 - 2 * core))

    def x_copy(other):
        return pltpu.make_async_remote_copy(
            src_ref=x_send.at[other, pl.ds(0, rows + 1)],
            dst_ref=x_recv.at[me, pl.ds(0, rows + 1)],
            send_sem=x_send_sem.at[other],
            recv_sem=x_recv_sem.at[me],
            device_id={"virt": other},
            device_id_type=MESH,
        )

    def x_arrival(other):
        return pltpu.make_async_remote_copy(
            src_ref=x_send.at[other, pl.ds(0, rows + 1)],
            dst_ref=x_recv.at[other, pl.ds(0, rows + 1)],
            send_sem=x_send_sem.at[other],
            recv_sem=x_recv_sem.at[other],
            device_id={"virt": other},
            device_id_type=MESH,
        )

    def x_stay():
        return pltpu.make_async_copy(x_send.at[me], x_recv.at[me], local_sem.at[2])

    load_j.wait()
    j_targets(me, lambda copy: copy.start())
    load_i.wait()

    @pl.loop(0, rows // 32)
    def _(step):
        part = pl.ds(pl.multiple_of(step * 32, 32), 32)
        high, low = split(total[part, :])
        i_high[part, :] = high
        i_low[part, :] = low
        total[part, :] = jnp.zeros((32, depth), jnp.float32)

    width = energy_ref.shape[1]
    energy = energy_ref[...]
    twice = jnp.concatenate([energy, energy], axis=1)
    tall_energy = jnp.broadcast_to(twice, (LANES, LANES)).T[:width]
    for orbital in range(rows // width):
        row_ref[orbital * width:(orbital + 1) * width, :] = tall_energy - occ_i_ref[orbital]
    col_lane = lax.broadcasted_iota(jnp.int32, (8, LANES), 1)
    col_term = jnp.broadcast_to(twice, (8, LANES)) - jnp.where(
        col_lane < width, occ_j_ref[0], occ_j_ref[1]
    )

    @pl.loop(0, n)
    def _(other):
        x_send[other, pl.ds(rows, 8), :] = col_term

    def split_j(place, copies):
        per = LANES // 32

        @pl.loop(0, 2 * per)
        def _(step):
            from_rows = pl.ds(pl.multiple_of(lax.rem(step, per) * 32, 32), 32)
            high, low = split(j_all[2 * place + step // per, from_rows, :])
            base = pl.multiple_of(step * 32, 32)
            j_parts[pl.ds(base, 32), :] = high
            j_parts[pl.ds(pair + base, 32), :] = low
            if copies == 3:
                j_parts[pl.ds(2 * pair + base, 32), :] = high

    toward = jnp.where(2 * z >= levels, -1, 1)

    def visit(step):
        level = step // 4
        kind = lax.rem(step // 2, 2)
        sign = lax.rem(step, 2)
        distance = level - kind
        at_y = jnp.where(kind == 0, y, columns - 1 - y)

        def on(way):
            at_z = z + toward * (1 - 2 * way) * distance
            valid = jnp.logical_and(distance >= 0, jnp.logical_and(at_z >= 0, at_z < levels))
            valid = jnp.logical_and(valid, jnp.logical_or(distance > 0, way == 0))
            if columns == 1:
                valid = jnp.logical_and(valid, kind == 0)
            return valid, at_z * columns + at_y

        return on, sign

    visits = 4 * (levels + columns - 1)

    @pl.loop(0, visits)
    def _(step):
        on, sign = visit(step)

        @pl.when(sign == 0)
        def _():
            for way in range(2):
                valid, place = on(way)
                origin = 2 * place + core

                @pl.when(jnp.logical_and(valid, origin != me))
                def _():
                    j_copy(origin, 0, me).wait_recv()
                    j_targets(origin, lambda copy: copy.start())

        valid, place = on(sign)

        @pl.when(valid)
        def _():
            j_copy(2 * place + 1 - core, 0, me).wait_recv()
            split_j(place, 2)
            lane = lax.broadcasted_iota(jnp.int32, (LANES // 2, LANES), 1)
            half = LANES // 2
            contract = (((1,), (1,)), ((), ()))

            @pl.loop(0, rows // tall)
            def _(block):
                start = pl.multiple_of(block * tall, tall)
                high, low = i_high[pl.ds(start, tall), :], i_low[pl.ds(start, tall), :]
                j_high, j_low = j_parts[pl.ds(0, pair), :], j_parts[pl.ds(pair, pair), :]
                dot = functools.partial(
                    lax.dot_general, dimension_numbers=contract,
                    preferred_element_type=jnp.float32,
                )
                block_pair = dot(high, j_high) + (dot(high, j_low) + dot(low, j_high))
                direct[place, pl.ds(start, tall), :] = block_pair
                for side in range(2):
                    for group in range(tall // LANES):
                        tile = block_pair[
                            group * LANES:(group + 1) * LANES, side * LANES:(side + 1) * LANES
                        ]
                        turned = tile.T
                        moved = pltpu.roll(turned, half, 1)
                        first = jnp.where(lane < half, turned[:half], moved[half:])
                        second = jnp.where(lane < half, moved[:half], turned[half:])
                        base = start + group * LANES
                        x_send[2 * place + side, pl.ds(base, half), :] = first
                        x_send[2 * place + side, pl.ds(base + half, half), :] = second

            for side in range(2):
                other = 2 * place + side

                @pl.when(other != me)
                def _():
                    x_copy(other).start()

                @pl.when(other == me)
                def _():
                    x_stay().start()

    def await_blocks(place):
        for side in range(2):
            other = 2 * place + side

            @pl.when(other != me)
            def _():
                x_arrival(other).wait_recv()

            @pl.when(other == me)
            def _():
                x_stay().wait()

    def amplitudes(place, part):
        for side in range(2):
            other = 2 * place + side
            lanes = slice(side * LANES, (side + 1) * LANES)
            swapped = x_recv[other, part, :]
            own = direct[place, part, lanes]
            denominator = row_ref[part, :] + x_recv[other, pl.ds(rows, 1), :]
            high, low = split((swapped - 2.0 * own) / denominator)
            amp_parts[part, side * LANES:(side + 1) * LANES] = high
            amp_parts[part, pair + side * LANES:pair + (side + 1) * LANES] = high
            amp_parts[part, 2 * pair + side * LANES:2 * pair + (side + 1) * LANES] = low

    farthest = jnp.maximum(z, levels - 1 - z)
    back = z - toward * farthest
    forth = z + toward * farthest
    back_valid = jnp.logical_and(back >= 0, back < levels)
    last_place = jnp.where(back_valid, back, forth) * columns + columns - 1 - y

    @pl.loop(0, visits)
    def _(step):
        on, sign = visit(step)
        valid, place = on(sign)

        @pl.when(jnp.logical_and(valid, place != last_place))
        def _():
            split_j(place, 3)
            await_blocks(place)

            @pl.loop(0, rows // tall)
            def _(block):
                part = pl.ds(pl.multiple_of(block * tall, tall), tall)
                amplitudes(place, part)

                @pl.loop(0, depth // wide)
                def _(strip):
                    at = pl.ds(pl.multiple_of(strip * wide, wide), wide)
                    total[part, at] += jnp.dot(
                        amp_parts[part, :], j_parts[:, at], preferred_element_type=jnp.float32
                    )

    store = pltpu.make_async_copy(total, part_ref, local_sem.at[0])
    store.start()
    split_j(last_place, 3)
    store_j = pltpu.make_async_copy(j_parts, last_j_ref, local_sem.at[1])
    store_j.start()

    @pl.loop(0, n)
    def _(other):
        j_targets(other, lambda copy: copy.wait_send())

    await_blocks(last_place)

    def store_amp(block):
        part = pl.ds(pl.multiple_of(block * tall, tall), tall)
        return pltpu.make_async_copy(amp_parts.at[part], amp_ref.at[part], amp_sem.at[block])

    @pl.loop(0, rows // tall)
    def _(block):
        amplitudes(last_place, pl.ds(pl.multiple_of(block * tall, tall), tall))
        store_amp(block).start()

    @pl.loop(0, n)
    def _(other):
        @pl.when(other != me)
        def _():
            x_copy(other).wait_send()

    store.wait()
    store_j.wait()

    @pl.loop(0, rows // tall)
    def _(block):
        store_amp(block).wait()


def finish(part_ref, amp_ref, j_ref, out_ref):
    wide = 512
    for start in range(0, part_ref.shape[1], wide):
        at = slice(start, start + wide)
        out_ref[:, at] = part_ref[:, at] + jnp.dot(
            amp_ref[...], j_ref[:, at], preferred_element_type=jnp.float32
        )


def fused(columns, i_factors, j_factors, occ_i, occ_j, virt_energy):
    n = lax.axis_size("virt")
    ni, width, depth = i_factors.shape
    nj = j_factors.shape[0]
    rows = ni * width
    anywhere = pl.BlockSpec(memory_space=pl.ANY)
    vmem = pl.BlockSpec(memory_space=pltpu.VMEM)
    f32, bf16 = jnp.float32, jnp.bfloat16
    dma = pltpu.SemaphoreType.DMA
    smem = pl.BlockSpec(memory_space=pltpu.SMEM)
    part, amp, last_j = pl.pallas_call(
        functools.partial(kernel, n, columns),
        out_shape=(
            jax.ShapeDtypeStruct((rows, depth), f32),
            jax.ShapeDtypeStruct((rows, 6 * LANES), bf16),
            jax.ShapeDtypeStruct((6 * LANES, depth), bf16),
        ),
        in_specs=[anywhere, anywhere, vmem, smem, smem],
        out_specs=(anywhere, anywhere, anywhere),
        scratch_shapes=[
            pltpu.VMEM((rows, depth), bf16),
            pltpu.VMEM((rows, depth), bf16),
            pltpu.VMEM((n, LANES, depth), f32),
            pltpu.VMEM((n // 2, rows, 2 * LANES), f32),
            pltpu.VMEM((n, rows + 8, LANES), f32),
            pltpu.VMEM((n, rows + 8, LANES), f32),
            pltpu.VMEM((rows, depth), f32),
            pltpu.VMEM((6 * LANES, depth), bf16),
            pltpu.VMEM((rows, 6 * LANES), bf16),
            pltpu.VMEM((rows, LANES), f32),
            dma((3,)),
            dma((n, 4)),
            dma((n,)),
            dma((n,)),
            dma((n,)),
            dma((rows // 256,)),
        ],
        compiler_params=pltpu.CompilerParams(
            collective_id=0, has_side_effects=True, vmem_limit_bytes=67043328
        ),
        name="pair_exchange",
    )(
        i_factors.reshape(rows, depth), j_factors.reshape(nj * width, depth),
        virt_energy.reshape(1, width), occ_i, occ_j,
    )
    tall = 128
    out = pl.pallas_call(
        finish,
        out_shape=jax.ShapeDtypeStruct((rows, depth), f32),
        grid=(rows // tall,),
        in_specs=[
            pl.BlockSpec((tall, depth), lambda step: (step, 0)),
            pl.BlockSpec((tall, 6 * LANES), lambda step: (step, 0)),
            pl.BlockSpec((6 * LANES, depth), lambda step: (0, 0)),
        ],
        out_specs=pl.BlockSpec((tall, depth), lambda step: (step, 0)),
        name="last_block",
    )(part, amp, last_j)
    return out.reshape(i_factors.shape)


def transpose_blocks(pair_block, blocks):
    leading = pair_block.shape[:-2]
    height = pair_block.shape[-2]
    width = pair_block.shape[-1]
    parts = pair_block.reshape(leading + (height, blocks, height))
    moved = jnp.swapaxes(parts, -1, -3)
    return moved.reshape(leading + (height, width))


def general(i_factors, j_factors, occ_i, occ_j, virt_energy):
    blocks = lax.axis_size("virt")
    left_rows = i_factors.reshape(-1, i_factors.shape[2])
    density = jnp.zeros(i_factors.shape, jnp.float32)
    whole_energy = lax.all_gather(virt_energy, "virt", axis=0, tiled=True)
    for index in range(j_factors.shape[0]):
        whole_rows = lax.all_gather(j_factors[index], "virt", axis=0, tiled=True)
        pair_block = jnp.dot(left_rows, whole_rows.T, precision=lax.Precision.HIGHEST)
        pair_block = pair_block.reshape(i_factors.shape[0], i_factors.shape[1], whole_rows.shape[0])
        swapped = lax.all_to_all(
            transpose_blocks(pair_block, blocks), "virt", split_axis=2, concat_axis=2, tiled=True
        )
        denominator = (
            virt_energy[None, :, None]
            + whole_energy[None, None, :]
            - occ_i[:, None, None]
            - occ_j[index]
        )
        amplitude = (swapped - 2.0 * pair_block) / denominator
        density = density + jnp.einsum(
            "iab,bp->iap", amplitude, whole_rows, precision=lax.Precision.HIGHEST
        )
    return density


def chip_columns(mesh):
    group = list(mesh.devices.reshape(-1, mesh.shape["virt"])[0])
    if len(group) % 2:
        return 0
    chips = group[::2]
    heights = len({getattr(device, "coords", (0, 0, place))[2] for place, device in enumerate(chips)})
    columns, left = divmod(len(chips), heights)
    return columns if left == 0 and columns in (1, 2) else 0


def body(columns, i_factors, j_factors, occ_i, occ_j, virt_energy):
    ni, width, depth = i_factors.shape
    nj = j_factors.shape[0]
    fits = nj == 2 and nj * width == LANES and (ni * width) % 256 == 0 and depth % 512 == 0
    n = lax.axis_size("virt")
    room = 4 * ni * width * depth * 2 + 4 * n * LANES * (depth + 3 * (ni * width + 8))
    if columns and fits and room < 58 * 2**20:
        return fused(columns, i_factors, j_factors, occ_i, occ_j, virt_energy)
    return general(i_factors, j_factors, occ_i, occ_j, virt_energy)


def solution(mesh):
    placed = (
        P("conf", "virt", None),
        P("conf", "virt", None),
        P("conf"),
        P("conf"),
        P(("conf", "virt")),
    )
    return jax.shard_map(
        functools.partial(body, chip_columns(mesh)),
        mesh=mesh, in_specs=placed, out_specs=P("conf", "virt", None), check_vma=False,
    )
```

```python
import functools

import jax
import jax.numpy as jnp
from jax import lax
from jax.experimental import pallas as pl
from jax.experimental.pallas import tpu as pltpu
from jax.sharding import PartitionSpec as P

LANES = 128
MESH = pl.DeviceIdType.MESH


def split(value):
    high = value.astype(jnp.bfloat16)
    low = (value - high.astype(jnp.float32)).astype(jnp.bfloat16)
    return high, low


def kernel(
    n, columns, i_ref, j_ref, energy_ref, occ_i_ref, occ_j_ref, part_ref, amp_ref, last_j_ref,
    i_high, i_low, j_all, direct, x_send, x_recv, total, j_parts, amp_parts, row_ref,
    local_sem, j_send_sem, j_recv_sem, x_send_sem, x_recv_sem, amp_sem,
):
    levels = n // 2 // columns
    me = lax.axis_index("virt")
    core = lax.rem(me, 2)
    chip = me // 2
    y = lax.rem(chip, columns)
    z = chip // columns
    rows, depth = i_ref.shape
    pair = 2 * LANES
    tall = 256
    wide = 512

    load_i = pltpu.make_async_copy(i_ref, total, local_sem.at[0])
    load_i.start()
    load_j = pltpu.make_async_copy(j_ref, j_all.at[me], local_sem.at[1])
    load_j.start()

    barrier = pltpu.get_barrier_semaphore()

    @pl.loop(1, n)
    def _(step):
        pl.semaphore_signal(
            barrier, inc=1, device_id={"virt": lax.rem(me + step, n)}, device_id_type=MESH
        )

    pl.semaphore_wait(barrier, n - 1)

    def j_copy(origin, way, device):
        return pltpu.make_async_remote_copy(
            src_ref=j_all.at[origin],
            dst_ref=j_all.at[origin],
            send_sem=j_send_sem.at[origin, way],
            recv_sem=j_recv_sem.at[origin],
            device_id={"virt": device},
            device_id_type=MESH,
        )

    def j_targets(origin, act):
        place = origin // 2
        same_core = lax.rem(origin, 2) == core
        in_column = jnp.logical_and(same_core, lax.rem(place, columns) == y)
        from_z = place // columns

        @pl.when(jnp.logical_and(in_column, jnp.logical_and(z >= from_z, z + 1 < levels)))
        def _():
            act(j_copy(origin, 0, me + 2 * columns))

        @pl.when(jnp.logical_and(in_column, jnp.logical_and(z <= from_z, z > 0)))
        def _():
            act(j_copy(origin, 1, me - 2 * columns))

        if columns == 2:
            @pl.when(in_column)
            def _():
                act(j_copy(origin, 2, me + 2 * (1 - 2 * y)))

        @pl.when(same_core)
        def _():
            act(j_copy(origin, 3, me + 1 - 2 * core))

    def x_copy(other):
        return pltpu.make_async_remote_copy(
            src_ref=x_send.at[other, pl.ds(0, rows + 1)],
            dst_ref=x_recv.at[me, pl.ds(0, rows + 1)],
            send_sem=x_send_sem.at[other],
            recv_sem=x_recv_sem.at[me],
            device_id={"virt": other},
            device_id_type=MESH,
        )

    def x_arrival(other):
        return pltpu.make_async_remote_copy(
            src_ref=x_send.at[other, pl.ds(0, rows + 1)],
            dst_ref=x_recv.at[other, pl.ds(0, rows + 1)],
            send_sem=x_send_sem.at[other],
            recv_sem=x_recv_sem.at[other],
            device_id={"virt": other},
            device_id_type=MESH,
        )

    def x_stay():
        return pltpu.make_async_copy(x_send.at[me], x_recv.at[me], local_sem.at[2])

    load_j.wait()
    j_targets(me, lambda copy: copy.start())
    load_i.wait()

    @pl.loop(0, rows // 32)
    def _(step):
        part = pl.ds(pl.multiple_of(step * 32, 32), 32)
        high, low = split(total[part, :])
        i_high[part, :] = high
        i_low[part, :] = low
        total[part, :] = jnp.zeros((32, depth), jnp.float32)

    width = energy_ref.shape[1]
    energy = energy_ref[...]
    twice = jnp.concatenate([energy, energy], axis=1)
    tall_energy = jnp.broadcast_to(twice, (LANES, LANES)).T[:width]
    for orbital in range(rows // width):
        row_ref[orbital * width:(orbital + 1) * width, :] = tall_energy - occ_i_ref[orbital]
    col_lane = lax.broadcasted_iota(jnp.int32, (8, LANES), 1)
    col_term = jnp.broadcast_to(twice, (8, LANES)) - jnp.where(
        col_lane < width, occ_j_ref[0], occ_j_ref[1]
    )

    @pl.loop(0, n)
    def _(other):
        x_send[other, pl.ds(rows, 8), :] = col_term

    def split_j(place, copies):
        per = LANES // 32

        @pl.loop(0, 2 * per)
        def _(step):
            from_rows = pl.ds(pl.multiple_of(lax.rem(step, per) * 32, 32), 32)
            high, low = split(j_all[2 * place + step // per, from_rows, :])
            base = pl.multiple_of(step * 32, 32)
            j_parts[pl.ds(base, 32), :] = high
            j_parts[pl.ds(pair + base, 32), :] = low
            if copies == 3:
                j_parts[pl.ds(2 * pair + base, 32), :] = high

    toward = jnp.where(2 * z >= levels, -1, 1)

    def visit(step):
        level = step // 4
        kind = lax.rem(step // 2, 2)
        sign = lax.rem(step, 2)
        distance = level - kind
        at_y = jnp.where(kind == 0, y, columns - 1 - y)

        def on(way):
            at_z = z + toward * (1 - 2 * way) * distance
            valid = jnp.logical_and(distance >= 0, jnp.logical_and(at_z >= 0, at_z < levels))
            valid = jnp.logical_and(valid, jnp.logical_or(distance > 0, way == 0))
            if columns == 1:
                valid = jnp.logical_and(valid, kind == 0)
            return valid, at_z * columns + at_y

        return on, sign

    visits = 4 * (levels + columns - 1)

    @pl.loop(0, visits)
    def _(step):
        on, sign = visit(step)

        @pl.when(sign == 0)
        def _():
            for way in range(2):
                valid, place = on(way)
                origin = 2 * place + core

                @pl.when(jnp.logical_and(valid, origin != me))
                def _():
                    j_copy(origin, 0, me).wait_recv()
                    j_targets(origin, lambda copy: copy.start())

        valid, place = on(sign)

        @pl.when(valid)
        def _():
            j_copy(2 * place + 1 - core, 0, me).wait_recv()
            split_j(place, 2)
            lane = lax.broadcasted_iota(jnp.int32, (LANES // 2, LANES), 1)
            half = LANES // 2
            contract = (((1,), (1,)), ((), ()))

            @pl.loop(0, rows // tall)
            def _(block):
                start = pl.multiple_of(block * tall, tall)
                high, low = i_high[pl.ds(start, tall), :], i_low[pl.ds(start, tall), :]
                j_high, j_low = j_parts[pl.ds(0, pair), :], j_parts[pl.ds(pair, pair), :]
                dot = functools.partial(
                    lax.dot_general, dimension_numbers=contract,
                    preferred_element_type=jnp.float32,
                )
                block_pair = dot(high, j_high) + (dot(high, j_low) + dot(low, j_high))
                direct[place, pl.ds(start, tall), :] = block_pair
                for side in range(2):
                    for group in range(tall // LANES):
                        tile = block_pair[
                            group * LANES:(group + 1) * LANES, side * LANES:(side + 1) * LANES
                        ]
                        turned = tile.T
                        moved = pltpu.roll(turned, half, 1)
                        first = jnp.where(lane < half, turned[:half], moved[half:])
                        second = jnp.where(lane < half, moved[:half], turned[half:])
                        base = start + group * LANES
                        x_send[2 * place + side, pl.ds(base, half), :] = first
                        x_send[2 * place + side, pl.ds(base + half, half), :] = second

            for side in range(2):
                other = 2 * place + side

                @pl.when(other != me)
                def _():
                    x_copy(other).start()

                @pl.when(other == me)
                def _():
                    x_stay().start()

    def await_blocks(place):
        for side in range(2):
            other = 2 * place + side

            @pl.when(other != me)
            def _():
                x_arrival(other).wait_recv()

            @pl.when(other == me)
            def _():
                x_stay().wait()

    def amplitudes(place, part):
        for side in range(2):
            other = 2 * place + side
            lanes = slice(side * LANES, (side + 1) * LANES)
            swapped = x_recv[other, part, :]
            own = direct[place, part, lanes]
            denominator = row_ref[part, :] + x_recv[other, pl.ds(rows, 1), :]
            high, low = split((swapped - 2.0 * own) / denominator)
            amp_parts[part, side * LANES:(side + 1) * LANES] = high
            amp_parts[part, pair + side * LANES:pair + (side + 1) * LANES] = high
            amp_parts[part, 2 * pair + side * LANES:2 * pair + (side + 1) * LANES] = low

    farthest = jnp.maximum(z, levels - 1 - z)
    back = z - toward * farthest
    forth = z + toward * farthest
    back_valid = jnp.logical_and(back >= 0, back < levels)
    last_place = jnp.where(back_valid, back, forth) * columns + columns - 1 - y

    @pl.loop(0, visits)
    def _(step):
        on, sign = visit(step)
        valid, place = on(sign)

        @pl.when(jnp.logical_and(valid, place != last_place))
        def _():
            split_j(place, 3)
            await_blocks(place)

            @pl.loop(0, rows // tall)
            def _(block):
                amplitudes(place, pl.ds(pl.multiple_of(block * tall, tall), tall))

            @pl.loop(0, depth // pair)
            def _(strip):
                at = pl.ds(pl.multiple_of(strip * pair, pair), pair)
                total[:, at] += jnp.dot(
                    amp_parts[...], j_parts[:, at], preferred_element_type=jnp.float32
                )

    store = pltpu.make_async_copy(total, part_ref, local_sem.at[0])
    store.start()
    split_j(last_place, 3)
    store_j = pltpu.make_async_copy(j_parts, last_j_ref, local_sem.at[1])
    store_j.start()

    @pl.loop(0, n)
    def _(other):
        j_targets(other, lambda copy: copy.wait_send())

    await_blocks(last_place)

    def store_amp(block):
        part = pl.ds(pl.multiple_of(block * tall, tall), tall)
        return pltpu.make_async_copy(amp_parts.at[part], amp_ref.at[part], amp_sem.at[block])

    @pl.loop(0, rows // tall)
    def _(block):
        amplitudes(last_place, pl.ds(pl.multiple_of(block * tall, tall), tall))
        store_amp(block).start()

    @pl.loop(0, n)
    def _(other):
        @pl.when(other != me)
        def _():
            x_copy(other).wait_send()

    store.wait()
    store_j.wait()

    @pl.loop(0, rows // tall)
    def _(block):
        store_amp(block).wait()


def finish(part_ref, amp_ref, j_ref, out_ref):
    wide = 256
    for start in range(0, part_ref.shape[1], wide):
        at = slice(start, start + wide)
        out_ref[:, at] = part_ref[:, at] + jnp.dot(
            amp_ref[...], j_ref[:, at], preferred_element_type=jnp.float32
        )


def fused(columns, i_factors, j_factors, occ_i, occ_j, virt_energy):
    n = lax.axis_size("virt")
    ni, width, depth = i_factors.shape
    nj = j_factors.shape[0]
    rows = ni * width
    anywhere = pl.BlockSpec(memory_space=pl.ANY)
    vmem = pl.BlockSpec(memory_space=pltpu.VMEM)
    f32, bf16 = jnp.float32, jnp.bfloat16
    dma = pltpu.SemaphoreType.DMA
    smem = pl.BlockSpec(memory_space=pltpu.SMEM)
    part, amp, last_j = pl.pallas_call(
        functools.partial(kernel, n, columns),
        out_shape=(
            jax.ShapeDtypeStruct((rows, depth), f32),
            jax.ShapeDtypeStruct((rows, 6 * LANES), bf16),
            jax.ShapeDtypeStruct((6 * LANES, depth), bf16),
        ),
        in_specs=[anywhere, anywhere, vmem, smem, smem],
        out_specs=(anywhere, anywhere, anywhere),
        scratch_shapes=[
            pltpu.VMEM((rows, depth), bf16),
            pltpu.VMEM((rows, depth), bf16),
            pltpu.VMEM((n, LANES, depth), f32),
            pltpu.VMEM((n // 2, rows, 2 * LANES), f32),
            pltpu.VMEM((n, rows + 8, LANES), f32),
            pltpu.VMEM((n, rows + 8, LANES), f32),
            pltpu.VMEM((rows, depth), f32),
            pltpu.VMEM((6 * LANES, depth), bf16),
            pltpu.VMEM((rows, 6 * LANES), bf16),
            pltpu.VMEM((rows, LANES), f32),
            dma((3,)),
            dma((n, 4)),
            dma((n,)),
            dma((n,)),
            dma((n,)),
            dma((rows // 256,)),
        ],
        compiler_params=pltpu.CompilerParams(
            collective_id=0, has_side_effects=True, vmem_limit_bytes=67043328
        ),
        name="pair_exchange",
    )(
        i_factors.reshape(rows, depth), j_factors.reshape(nj * width, depth),
        virt_energy.reshape(1, width), occ_i, occ_j,
    )
    tall = 256
    out = pl.pallas_call(
        finish,
        out_shape=jax.ShapeDtypeStruct((rows, depth), f32),
        grid=(rows // tall,),
        in_specs=[
            pl.BlockSpec((tall, depth), lambda step: (step, 0)),
            pl.BlockSpec((tall, 6 * LANES), lambda step: (step, 0)),
            pl.BlockSpec((6 * LANES, depth), lambda step: (0, 0)),
        ],
        out_specs=pl.BlockSpec((tall, depth), lambda step: (step, 0)),
        name="last_block",
    )(part, amp, last_j)
    return out.reshape(i_factors.shape)


def transpose_blocks(pair_block, blocks):
    leading = pair_block.shape[:-2]
    height = pair_block.shape[-2]
    width = pair_block.shape[-1]
    parts = pair_block.reshape(leading + (height, blocks, height))
    moved = jnp.swapaxes(parts, -1, -3)
    return moved.reshape(leading + (height, width))


def general(i_factors, j_factors, occ_i, occ_j, virt_energy):
    blocks = lax.axis_size("virt")
    left_rows = i_factors.reshape(-1, i_factors.shape[2])
    density = jnp.zeros(i_factors.shape, jnp.float32)
    whole_energy = lax.all_gather(virt_energy, "virt", axis=0, tiled=True)
    for index in range(j_factors.shape[0]):
        whole_rows = lax.all_gather(j_factors[index], "virt", axis=0, tiled=True)
        pair_block = jnp.dot(left_rows, whole_rows.T, precision=lax.Precision.HIGHEST)
        pair_block = pair_block.reshape(i_factors.shape[0], i_factors.shape[1], whole_rows.shape[0])
        swapped = lax.all_to_all(
            transpose_blocks(pair_block, blocks), "virt", split_axis=2, concat_axis=2, tiled=True
        )
        denominator = (
            virt_energy[None, :, None]
            + whole_energy[None, None, :]
            - occ_i[:, None, None]
            - occ_j[index]
        )
        amplitude = (swapped - 2.0 * pair_block) / denominator
        density = density + jnp.einsum(
            "iab,bp->iap", amplitude, whole_rows, precision=lax.Precision.HIGHEST
        )
    return density


def chip_columns(mesh):
    group = list(mesh.devices.reshape(-1, mesh.shape["virt"])[0])
    if len(group) % 2:
        return 0
    chips = group[::2]
    heights = len({getattr(device, "coords", (0, 0, place))[2] for place, device in enumerate(chips)})
    columns, left = divmod(len(chips), heights)
    return columns if left == 0 and columns in (1, 2) else 0


def body(columns, i_factors, j_factors, occ_i, occ_j, virt_energy):
    ni, width, depth = i_factors.shape
    nj = j_factors.shape[0]
    fits = nj == 2 and nj * width == LANES and (ni * width) % 256 == 0 and depth % 512 == 0
    n = lax.axis_size("virt")
    room = 4 * ni * width * depth * 2 + 4 * n * LANES * (depth + 3 * (ni * width + 8))
    if columns and fits and room < 58 * 2**20:
        return fused(columns, i_factors, j_factors, occ_i, occ_j, virt_energy)
    return general(i_factors, j_factors, occ_i, occ_j, virt_energy)


def solution(mesh):
    placed = (
        P("conf", "virt", None),
        P("conf", "virt", None),
        P("conf"),
        P("conf"),
        P(("conf", "virt")),
    )
    return jax.shard_map(
        functools.partial(body, chip_columns(mesh)),
        mesh=mesh, in_specs=placed, out_specs=P("conf", "virt", None), check_vma=False,
    )
```
